128 devices in a mesh: space: 8 (over z, core), mode: 16 (over y, x).
Axes of the slice: x: 4, y: 4, z: 4, core: 2. Of those that a mesh axis runs over, the one named last changes fastest.
Arguments:
- sqrt_factors: bfloat16 [512, 3, 384, 512], P('mode', None, 'space'), may hold values from -10 to 10
- model_error: bfloat16 [256, 3, 384, 512], P(None, None, ('space', 'mode')), may hold values from -6 to 6
- water_depth: float32 [384, 512], P('space'), may hold values from 0.5 to 2
- sea_mask: int32 [384, 512], P('space'), may hold values 0 or 1
- givens_transform: bfloat16 [768, 512], replicated, may hold values from -0.2 to 1.2
Outputs:
- reduced_modes: bfloat16 [512, 3, 384, 512], P('mode', None, 'space')
- gram_matrix: float32 [768, 768], P(('space', 'mode'))
- inflation: float32 [], replicated
The draws below stay inside these ranges and needn't reach their ends.
All inputs are finite; a program needn't handle non-finite values. No bound on the sum of `sea_mask` on one device may be relied on, other than what follows from the above.
Results may differ from the reference program's by a relative error of at most 0.0049.
Values may be sent and summed in bfloat16 or wider, within the bound.
A program may use at most 128 MiB of HBM per device.

```python
import math
import jax
import jax.numpy as jnp
from jax import lax

ERROR_FACTORS = 512
NOISE = 256
COLS = 512
LATITUDE_BANDS = 48
NROWS = 384
N_SPACE = 8


def draw_sqrt_factors(key, part):
    position = jnp.arange(NROWS, dtype=jnp.float32) / NROWS
    amplitude = 0.5 * jnp.exp(jnp.log(4.0) * position)
    array_shape = (ERROR_FACTORS, 3, NROWS, COLS)
    values = jnp.clip(jax.random.normal(key, array_shape, jnp.float32), -4.0, 4.0)
    return (values * amplitude[:, None]).astype(jnp.bfloat16)


def draw_givens_transform(key, part):
    columns = ERROR_FACTORS + NOISE
    identity = (jnp.arange(columns)[:, None] == jnp.arange(ERROR_FACTORS)[None, :]).astype(jnp.float32)
    values = jnp.clip(jax.random.normal(key, (columns, ERROR_FACTORS), jnp.float32), -3.0, 3.0)
    return (identity + 0.6 * values / math.sqrt(columns)).astype(jnp.bfloat16)


def set_ends(entries, stream_key, low, top_value):
    index_at = [jax.random.randint(jax.random.fold_in(stream_key, axis), (), 0, length) for axis, length in enumerate(entries.shape)]
    longest = entries.shape.index(max(entries.shape))
    beside = index_at[:longest] + [(index_at[longest] + 1) % entries.shape[longest]] + index_at[longest + 1:]
    return entries.at[tuple(index_at)].set(low).at[tuple(beside)].set(top_value)


def shard_levels(rng, dims, shards, smallest, largest):
    gain = 1.0
    for dim, parts in shards:
        draws = jax.random.uniform(jax.random.fold_in(jax.random.fold_in(rng, 6), dim), (parts,), jnp.float32, smallest / len(shards), largest / len(shards))
        gain = gain * jnp.repeat(jnp.exp(draws), dims[dim] // parts).reshape((-1,) + (1,) * (len(dims) - 1 - dim))
    return gain


def noise(own_key, extent, deviation, reach, cuts=(), held_as=jnp.bfloat16):
    drawn = jax.random.normal(own_key, extent, jnp.float32) * deviation
    if len(cuts) > 0:
        drawn = shard_levels(own_key, extent, cuts, -0.22, 0.18) * drawn
    return jnp.clip(drawn, min=-reach, max=reach).astype(held_as)


def setup_inputs(seed: int = 0) -> dict:
    seeds = jax.random.split(jax.random.key(seed), 6)
    return {
        "sqrt_factors": draw_sqrt_factors(jax.random.fold_in(seeds[5], 71), 0),
        "model_error": noise(seeds[1], (NOISE, 3, NROWS, COLS), 1.0, 6.0, ((2, 128),)),
        "water_depth": jnp.clip(jnp.exp(math.log(2.0) - 1.3862944 * jax.random.uniform(seeds[2], (NROWS, COLS), jnp.float32) ** shard_levels(seeds[2], (NROWS, COLS), ((0, 8),), -0.2, 0.2)), 0.5, 2.0),
        "sea_mask": set_ends((jax.random.randint(seeds[3], (NROWS, COLS), 0, 5) < 4).astype(jnp.int32), jax.random.fold_in(seeds[3], 1), 0, 1),
        "givens_transform": draw_givens_transform(jax.random.fold_in(seeds[5], 71), 0),
    }


flux_coef = 0.2
slope_coef = 0.2
turn_coef = 0.1
keep_coef = 0.95

def column_diff(field):
    widths = [(0, 0)] * (field.ndim - 1) + [(1, 1)]
    padded = jnp.pad(field, widths)
    return padded[..., 2:] - padded[..., :-2]

def advance(layered_surfaces, static):
    depth_cells = static[0]
    wet_cells = static[1]
    surface = layered_surfaces[:, 0]
    flow_east = layered_surfaces[:, 1]
    flow_north = layered_surfaces[:, 2]
    flux_east = depth_cells * flow_east
    flux_north = depth_cells * flow_north
    divergence = column_diff(flux_east[:, 1:-1]) + (flux_north[:, 2:] - flux_north[:, :-2])
    surface_new = wet_cells[1:-1] * (surface[:, 1:-1] - flux_coef * divergence)
    slope_east = column_diff(surface_new[:, 1:-1])
    slope_north = surface_new[:, 2:] - surface_new[:, :-2]
    wet_inner = wet_cells[2:-2]
    east_inner = flow_east[:, 2:-2]
    north_inner = flow_north[:, 2:-2]
    east_new = wet_inner * (keep_coef * east_inner + turn_coef * north_inner - slope_coef * slope_east)
    north_new = wet_inner * (keep_coef * north_inner - turn_coef * east_inner - slope_coef * slope_north)
    return (jnp.stack([surface_new[:, 1:-1], east_new, north_new], axis=1), static[:, 2:-2])

def reference(sqrt_factors, model_error, water_depth, sea_mask, givens_transform):
    static = jnp.stack([water_depth, sea_mask.astype(jnp.float32)])
    static_pad = jnp.pad(static, ((0, 0), (2, 2), (0, 0)))

    def prior_factor_set(factor_collection):
        layered_surfaces = factor_collection.astype(jnp.float32)
        for iteration in range(2):
            padded = jnp.pad(layered_surfaces, ((0, 0), (0, 0), (2, 2), (0, 0)))
            layered_surfaces, unused = advance(padded, static_pad)
        return layered_surfaces.astype(jnp.bfloat16)
    banded_factors = sqrt_factors.reshape((16, ERROR_FACTORS // 16) + sqrt_factors.shape[1:])
    prior_factors = lax.map(prior_factor_set, banded_factors).reshape(sqrt_factors.shape)
    rotation_wide = givens_transform.astype(jnp.float32)
    transform_head = rotation_wide[:ERROR_FACTORS]
    rotation_low = rotation_wide[ERROR_FACTORS:]
    inner_sum_fn = (((1,), (1,)), ((), ()))
    pairwise_entries = (((0,), (0,)), ((), ()))
    largest_level = lax.Precision.HIGHEST

    def partition_latitudes(partition_place):
        first_latitude = (partition_place * LATITUDE_BANDS).astype(jnp.int32)
        prior_latitudes = lax.dynamic_slice_in_dim(prior_factors, first_latitude, LATITUDE_BANDS, 2).astype(jnp.float32).reshape(ERROR_FACTORS, -1)
        model_fault_part = lax.dynamic_slice_in_dim(model_error, first_latitude, LATITUDE_BANDS, 2).astype(jnp.float32).reshape(NOISE, -1)
        return (prior_latitudes, model_fault_part)

    def gram_step(partition_place, carry):
        prior_latitudes, model_fault_part = partition_latitudes(partition_place)
        prior_moments = lax.dot_general(prior_latitudes, prior_latitudes, inner_sum_fn, precision=largest_level)
        mixed_moments = lax.dot_general(prior_latitudes, model_fault_part, inner_sum_fn, precision=largest_level)
        error_gram = lax.dot_general(model_fault_part, model_fault_part, inner_sum_fn, precision=largest_level)
        upper = jnp.concatenate([prior_moments, mixed_moments], 1)
        lower = jnp.concatenate([mixed_moments.T, error_gram], 1)
        return carry + jnp.concatenate([upper, lower], 0)
    summed = lax.fori_loop(0, N_SPACE, gram_step, jnp.zeros((ERROR_FACTORS + NOISE, ERROR_FACTORS + NOISE), jnp.float32))
    cell_count = 3.0 * NROWS * COLS
    gram_matrix = summed / cell_count
    trace_full = jnp.trace(gram_matrix)
    trace_kept = jnp.sum(jnp.dot(gram_matrix, rotation_wide, precision=largest_level) * rotation_wide)
    inflation = jnp.sqrt(trace_full / trace_kept)

    def rotate_step(partition_place, carry):
        prior_latitudes, model_fault_part = partition_latitudes(partition_place)
        truncated_factors = lax.dot_general(transform_head, prior_latitudes, pairwise_entries, precision=largest_level)
        truncated_factors = truncated_factors + lax.dot_general(rotation_low, model_fault_part, pairwise_entries, precision=largest_level)
        scaled = (inflation * truncated_factors).reshape(ERROR_FACTORS, 3, LATITUDE_BANDS, COLS).astype(jnp.bfloat16)
        first_latitude = (partition_place * LATITUDE_BANDS).astype(jnp.int32)
        return lax.dynamic_update_slice_in_dim(carry, scaled, first_latitude, 2)
    reduced_modes = lax.fori_loop(0, N_SPACE, rotate_step, jnp.zeros(sqrt_factors.shape, jnp.bfloat16))
    return (reduced_modes, gram_matrix, inflation)
```

```python
import jax
import jax.numpy as jnp
from jax import lax
from jax.experimental import pallas as pl
from jax.experimental.pallas import tpu as pltpu
from jax.sharding import PartitionSpec as P

flux_coef = 0.2
slope_coef = 0.2
turn_coef = 0.1
keep_coef = 0.95

MESH = pl.DeviceIdType.MESH
F32, BF16 = jnp.float32, jnp.bfloat16
NM, NZ, NY, NX = 16, 4, 4, 4
ROWS, COLS, LOCAL, PAIRS = 48, 512, 32, 9
MODES, NOISE, WIDE = 512, 256, 768
BAND, PIECE = WIDE // 8, 6
CELLS = 3.0 * 384 * 512
OFFSETS = [
    (0, 1), (1, 0), (0, 3), (3, 0), (1, 1), (0, 2), (3, 3), (2, 0),
    (1, 3), (1, 2), (3, 1), (3, 2), (2, 1), (2, 2), (2, 3),
]


def kernel(
    x_in, depth_in, mask_in, noise_in, rot_in, out, gram_out, infl_out,
    X, D, M, DN, DA, DB, W, S1, E1, N1, S2, F, L, R, G, G0, H, G1, K, G2, T,
    C0, C0r, C1, C2, gram_pad,
    sem_x, sem_load, sem_own, sem_halo_s, sem_halo_r, sem_fs, sem_fr, sem_bs, sem_br,
    sem_g0s, sem_g0r, sem_g1s, sem_g1r, sem_g2s, sem_g2r, sem_cs, sem_cr,
):
    space, mode = lax.axis_index("space"), lax.axis_index("mode")
    z, c = space // 2, lax.rem(space, 2)
    y, x = mode // NX, lax.rem(mode, NX)

    def mode_of(offset):
        return lax.rem(y + offset[0], NY) * NX + lax.rem(x + offset[1], NX)

    up, down = lax.rem(space + 1, 8), lax.rem(space + 7, 8)
    partner = z * 2 + (1 - c)
    far = lax.rem(space + 7 + 2 * c, 8)

    def z_of(k):
        return lax.rem(z + k, NZ)

    def remote(src, dst, send, recv, s, m):
        return pltpu.make_async_remote_copy(
            src_ref=src, dst_ref=dst, send_sem=send, recv_sem=recv,
            device_id=(s, m), device_id_type=MESH,
        )

    load_x = pltpu.make_async_copy(x_in, X.at[pl.ds(4, ROWS)], sem_x.at[0])
    load_d = pltpu.make_async_copy(depth_in, D.at[pl.ds(8, ROWS)], sem_x.at[1])
    load_m = pltpu.make_async_copy(mask_in, M.at[pl.ds(8, ROWS)], sem_x.at[2])
    load_e = pltpu.make_async_copy(noise_in, L.at[:, pl.ds(MODES, NOISE)], sem_load.at[0])
    load_t = pltpu.make_async_copy(rot_in, T, sem_load.at[1])
    for copy in (load_d, load_m, load_x, load_e, load_t):
        copy.start()

    barrier = pltpu.get_barrier_semaphore()
    peers = [(space, mode_of(o)) for o in OFFSETS]
    peers += [(partner, mode), (far, mode)] + [(z_of(k) * 2 + c, mode) for k in (1, 2, 3)]
    for s, m in peers:
        pl.semaphore_signal(barrier, inc=1, device_id=(s, m), device_id_type=MESH)
    pl.semaphore_wait(barrier, len(peers))

    halos = [
        remote(x_in.at[pl.ds(44, 4)], X.at[pl.ds(0, 4)], sem_halo_s.at[0], sem_halo_r.at[0], up, mode),
        remote(x_in.at[pl.ds(0, 4)], X.at[pl.ds(52, 4)], sem_halo_s.at[1], sem_halo_r.at[1], down, mode),
        remote(depth_in.at[pl.ds(40, 8)], D.at[pl.ds(0, 8)], sem_halo_s.at[2], sem_halo_r.at[2], up, mode),
        remote(depth_in.at[pl.ds(0, 8)], D.at[pl.ds(56, 8)], sem_halo_s.at[3], sem_halo_r.at[3], down, mode),
        remote(mask_in.at[pl.ds(40, 8)], M.at[pl.ds(0, 8)], sem_halo_s.at[4], sem_halo_r.at[4], up, mode),
        remote(mask_in.at[pl.ds(0, 8)], M.at[pl.ds(56, 8)], sem_halo_s.at[5], sem_halo_r.at[5], down, mode),
    ]
    for copy in halos:
        copy.start()

    lane = lax.broadcasted_iota(jnp.int32, (1, COLS), 1)
    first, last = lane == 0, lane == COLS - 1

    def prepare(lo, count, inside):
        rows = pl.ds(lo, count)
        depth = jnp.where(inside, D[rows, :] * flux_coef, 0.0)
        DN[rows, :] = depth
        DA[rows, :] = jnp.where(first, 0.0, depth)
        DB[rows, :] = jnp.where(last, 0.0, depth)
        W[rows, :] = jnp.where(inside, M[rows, :].astype(F32), 0.0)

    load_d.wait()
    load_m.wait()
    prepare(8, ROWS, True)
    load_x.wait()

    def halves(row):
        for g in range(2):
            row(pl.ds(16 * g, 16))

    def surface(q, g, s, e, n):
        t = q + 4
        flow = e(q, g)
        across = pltpu.roll(DA[pl.ds(t, 1), :] * flow, COLS - 1, 1) - pltpu.roll(
            DB[pl.ds(t, 1), :] * flow, 1, 1
        )
        along = DN[pl.ds(t + 1, 1), :] * n(q + 1, g) - DN[pl.ds(t - 1, 1), :] * n(q - 1, g)
        return W[pl.ds(t, 1), :] * (s(q, g) - (across + along))

    def flows(q, g, s, e, n):
        wet = W[pl.ds(q + 4, 1), :]
        here, east, north = s(q, g), e(q, g), n(q, g)
        slope = pltpu.roll(jnp.where(first, 0.0, here), COLS - 1, 1) - pltpu.roll(
            jnp.where(last, 0.0, here), 1, 1
        )
        east_new = wet * (keep_coef * east + turn_coef * north - slope_coef * slope)
        slope = s(q + 1, g) - s(q - 1, g)
        north_new = wet * (keep_coef * north - turn_coef * east - slope_coef * slope)
        return east_new, north_new

    def raw(field):
        return lambda q, g: X[q, field, g, :].astype(F32)

    def held(ref):
        return lambda q, g: ref[q, g, :]

    raws, firsts = [raw(f) for f in range(3)], [held(r) for r in (S1, E1, N1)]

    def surface_1(q):
        def row(g):
            S1[q, g, :] = surface(q, g, *raws)

        halves(row)

    def flows_1(q):
        def row(g):
            E1[q, g, :], N1[q, g, :] = flows(q, g, held(S1), raws[1], raws[2])

        halves(row)

    pl.loop(5, 51)(surface_1)
    pl.loop(6, 50)(flows_1)
    for copy in halos:
        copy.wait()
    prepare(0, 8, space > 0)
    prepare(56, 8, space < 7)

    @pl.loop(0, 8)
    def _(i):
        surface_1(jnp.where(i < 4, i + 1, i + 47))

    @pl.loop(0, 8)
    def _(i):
        flows_1(jnp.where(i < 4, i + 2, i + 46))

    def surface_2(q):
        def row(g):
            S2[q, g, :] = surface(q, g, *firsts)

        halves(row)

    surface_2(3)
    surface_2(52)

    @pl.loop(0, NM)
    def _(m):
        for i in range(3):
            q = 3 * m + i + 4

            def row(g, i=i, q=q):
                value = surface(q, g, *firsts)
                S2[q, g, :] = value
                F[m, i, g, :] = value.astype(BF16)

            halves(row)

    def send_pair(r):
        for o in OFFSETS:
            m = mode_of(o)
            remote(
                F.at[m, r], L.at[r, pl.ds(pl.multiple_of(mode * LOCAL, LOCAL), LOCAL)],
                sem_fs, sem_fr.at[r], space, m,
            ).start()

    pl.loop(0, 3)(send_pair)

    @pl.loop(0, NM)
    def _(m):
        for i in range(3):
            q = 3 * m + i + 4

            def row(g, i=i, q=q):
                east, north = flows(q, g, held(S2), firsts[1], firsts[2])
                F[m, 3 + i, g, :] = east.astype(BF16)
                F[m, 6 + i, g, :] = north.astype(BF16)

            halves(row)

    pl.loop(3, PAIRS)(send_pair)
    own = pl.ds(pl.multiple_of(mode * LOCAL, LOCAL), LOCAL)
    own_in = pltpu.make_async_copy(F.at[mode], L.at[:, own], sem_own.at[0])
    own_in.start()
    load_e.wait()
    load_t.wait()
    G[...] = jnp.zeros_like(G)
    C0[...] = jnp.zeros_like(C0)
    own_in.wait()

    def folded(value):
        value = value * value
        value = jnp.sum(value.reshape(-1, 8, value.shape[-1]), axis=0)
        return sum(value[:, 128 * k : 128 * (k + 1)] for k in range(value.shape[-1] // 128))

    @pl.loop(0, PAIRS)
    def _(r):
        pltpu.make_async_copy(
            L.at[r, pl.ds(0, MODES - LOCAL)], L.at[r, pl.ds(0, MODES - LOCAL)], sem_fr.at[r]
        ).wait()
        for b in range(2):
            part = pl.ds(256 * b, 256)
            rotated = jnp.dot(T[part, :], L[r], preferred_element_type=F32)
            C0[1] += folded(rotated)
            R[r, part, :] = rotated.astype(BF16)
        for o in OFFSETS:
            m = mode_of(o)
            remote(
                R.at[r, pl.ds(pl.multiple_of(m * LOCAL, LOCAL), LOCAL)], out.at[mode, r],
                sem_bs, sem_br, space, m,
            ).start()
        for b in range(3):
            part = pl.ds(256 * b, 256)
            block = L[r, part, :]
            C0[0] += folded(block.astype(F32))
            G[part, :] += lax.dot_general(
                block, L[r], (((1,), (1,)), ((), ())), preferred_element_type=F32
            )

    own_out = pltpu.make_async_copy(R.at[:, own], out.at[mode], sem_own.at[1])
    own_out.start()

    send_c0 = remote(C0, C0r, sem_cs.at[0], sem_cr.at[0], partner, mode)
    send_c0.start()
    for k in range(NZ):
        remote(
            G.at[pl.ds(pl.multiple_of((2 * k + 1 - c) * BAND, 8), BAND)], G0.at[k],
            sem_g0s, sem_g0r, partner, mode,
        ).start()
    send_c0.wait()
    C1[z] = C0[...] + C0r[...]
    for k in (1, 2, 3):
        remote(C1.at[z], C1.at[z], sem_cs.at[1], sem_cr.at[1], z_of(k) * 2 + c, mode).start()
    wait_c1 = remote(C1.at[pl.ds(0, 3)], C1.at[pl.ds(0, 3)], sem_cs.at[1], sem_cr.at[1], partner, mode)
    wait_c1.wait()
    C2[mode] = ((C1[0] + C1[1]) + C1[2]) + C1[3]
    for o in OFFSETS:
        remote(C2.at[mode], C2.at[mode], sem_cs.at[2], sem_cr.at[2], space, mode_of(o)).start()

    remote(G0, G0, sem_g0s, sem_g0r, partner, mode).wait()

    @pl.loop(0, NZ)
    def _(k):
        for b in range(4):
            rows = pl.ds(24 * b, 24)
            mine = pl.ds(pl.multiple_of((2 * k + c) * BAND + 24 * b, 8), 24)
            H[k, rows, :] = G[mine, :] + G0[k, rows, :]

    for k in (1, 2, 3):
        remote(H.at[z_of(k)], G1.at[k - 1], sem_g1s, sem_g1r, z_of(k) * 2 + c, mode).start()
    remote(G1, G1, sem_g1s, sem_g1r, partner, mode).wait()
    for m in range(NM):
        rows = pl.ds(PIECE * m, PIECE)
        total = (H[z, rows, :] + G1[0, rows, :]) + (G1[1, rows, :] + G1[2, rows, :])
        K[m, pl.ds(0, PIECE), :] = total
        K[m, pl.ds(PIECE, 2), :] = jnp.zeros((2, WIDE), F32)
    for o in OFFSETS:
        m = mode_of(o)
        remote(K.at[m], G2.at[mode], sem_g2s, sem_g2r, space, m).start()
    G2[mode] = K[mode]

    many = pl.ds(0, NM - 1)
    remote(C2.at[many], C2.at[many], sem_cs.at[2], sem_cr.at[2], partner, mode).wait()
    total = C2[0]
    for m in range(1, NM):
        total = total + C2[m]
    full = jnp.sum(jnp.sum(total[0], axis=0, keepdims=True), axis=1, keepdims=True)
    kept = jnp.sum(jnp.sum(total[1], axis=0, keepdims=True), axis=1, keepdims=True)
    infl_out[...] = jnp.broadcast_to(jnp.sqrt(full / kept), infl_out.shape)

    remote(G2.at[many], G2.at[many], sem_g2s, sem_g2r, partner, mode).wait()
    gram_pad[...] = jnp.sum(G2[...], axis=0) / CELLS
    gram_out[...] = gram_pad[pl.ds(0, PIECE), :]

    own_out.wait()
    remote(F.at[many], F.at[many], sem_fs, sem_br, partner, mode).wait_send()
    remote(out.at[many], out.at[many], sem_bs, sem_br, partner, mode).wait()


def shards(sqrt_factors, model_error, water_depth, sea_mask, givens_transform):
    fields = jnp.transpose(sqrt_factors, (2, 1, 0, 3))
    noise = jnp.transpose(model_error, (1, 2, 0, 3)).reshape(PAIRS, NOISE, COLS)
    rotation = givens_transform.T
    vmem, dma = pltpu.VMEM, pltpu.SemaphoreType.DMA
    anywhere = pl.BlockSpec(memory_space=pl.ANY)
    inside = pl.BlockSpec(memory_space=pltpu.VMEM)
    received, gram_rows, inflation = pl.pallas_call(
        kernel,
        out_shape=(
            jax.ShapeDtypeStruct((NM, PAIRS, LOCAL, COLS), BF16),
            jax.ShapeDtypeStruct((PIECE, WIDE), F32),
            jax.ShapeDtypeStruct((1, 128), F32),
        ),
        in_specs=[anywhere] * 5,
        out_specs=(anywhere, inside, inside),
        scratch_shapes=[
            vmem((ROWS + 8, 3, LOCAL, COLS), BF16),
            vmem((64, COLS), F32),
            vmem((64, COLS), jnp.int32),
            *[vmem((64, COLS), F32)] * 4,
            *[vmem((ROWS + 8, LOCAL, COLS), F32)] * 4,
            vmem((NM, PAIRS, LOCAL, COLS), BF16),
            vmem((PAIRS, WIDE, COLS), BF16),
            vmem((PAIRS, MODES, COLS), BF16),
            vmem((WIDE, WIDE), F32),
            vmem((NZ, BAND, WIDE), F32),
            vmem((NZ, BAND, WIDE), F32),
            vmem((NZ - 1, BAND, WIDE), F32),
            vmem((NM, 8, WIDE), F32),
            vmem((NM, 8, WIDE), F32),
            vmem((MODES, WIDE), BF16),
            vmem((2, 8, 128), F32),
            vmem((2, 8, 128), F32),
            vmem((NZ, 2, 8, 128), F32),
            vmem((NM, 2, 8, 128), F32),
            vmem((8, WIDE), F32),
            dma((3,)), dma((2,)), dma((2,)), dma((6,)), dma((6,)),
            dma, dma((PAIRS,)), dma, dma,
            dma, dma, dma, dma, dma, dma, dma((3,)), dma((3,)),
        ],
        compiler_params=pltpu.CompilerParams(
            collective_id=0, has_side_effects=True, vmem_limit_bytes=60 << 20
        ),
    )(fields, water_depth, sea_mask, noise, rotation)
    inflation = inflation[0, 0]
    scaled = (inflation * received.astype(F32)).astype(BF16)
    scaled = scaled.reshape(NM, 3, 3, LOCAL, COLS)
    reduced = jnp.transpose(scaled, (3, 1, 0, 2, 4)).reshape(sqrt_factors.shape)
    return (reduced, gram_rows, inflation)


def solution(mesh):
    in_specs = (
        P("mode", None, "space", None),
        P(None, None, ("space", "mode"), None),
        P("space", None),
        P("space", None),
        P(),
    )
    out_specs = (P("mode", None, "space", None), P(("space", "mode"), None), P())
    return jax.shard_map(shards, mesh=mesh, in_specs=in_specs, out_specs=out_specs, check_vma=False)
```
